128 devices in a mesh: shard: 128 (over z, x, y, core).
Axes of the slice: x: 4, y: 4, z: 4, core: 2. Of those that a mesh axis runs over, the one named last changes fastest.
Arguments:
- queries: bfloat16 [2048, 8, 9600], P('shard'), may hold values from -6 to 6
- index_videos: bfloat16 [16384, 8, 9600], P('shard'), may hold values from -6 to 6
- candidates: int32 [2048, 8], P('shard'), may hold values from 0 to 16383, as said below
- conv_one: bfloat16 [32, 1, 3, 3], replicated, may hold values from -2 to 2
- conv_two: bfloat16 [64, 32, 3, 3], replicated, may hold values from -0.375 to 0.375
- conv_three: bfloat16 [1, 64, 3, 3], replicated, may hold values from -0.25 to 0.25
Outputs:
- scores: float32 [2048, 8], P('shard')
The draws below stay inside these ranges and needn't reach their ends.
Inputs may be any that keep to these rules, and one draw needn't show every extreme that they name: `candidates`: each new video's 8 ids are distinct. The videos of id v are held by device v // 128. Of one device's pairs at most 2 name videos of one holder; in every draw some holders receive exactly 2 from every device.
All inputs are finite; a program needn't handle non-finite values.
Results may differ from the reference program's by a relative error of at most 0.0041.
Values may be sent and summed in bfloat16 or wider, within the bound.
A program may use at most 256 MiB of HBM per device.

```python
import math
import jax
import jax.numpy as jnp
from jax import lax

F = 8
R = 5
REGION_FEATURES = 1920
C1 = 32
C2 = 64
K = 8
Q_DEV = 16
IDX_DEV = 128
QUERIES = 2048
VIDEOS = 16384


def draw_candidates(key, part):
    devices = QUERIES // Q_DEV
    pairs = Q_DEV * K
    cap = max(2, (2 * pairs + devices - 1) // devices)
    hot_count = max(1, devices // 16)
    order = jax.random.permutation(jax.random.fold_in(key, 7), devices)
    hot = order[:hot_count]
    cold = order[hot_count:]
    cold_count = devices - hot_count

    def one_device(device):
        dkey = jax.random.fold_in(key, 1000 + device)
        cold_perm = cold[jax.random.permutation(jax.random.fold_in(dkey, 1), cold_count)]
        owners = jnp.concatenate([jnp.repeat(hot, cap), jnp.tile(cold_perm, cap)])[:pairs]
        ranks = jnp.concatenate([jnp.tile(jnp.arange(cap), hot_count), jnp.repeat(jnp.arange(cap), cold_count)])[:pairs]
        base = jax.random.randint(jax.random.fold_in(dkey, 2), (devices,), 0, IDX_DEV)
        slots = (base[owners] + ranks) % IDX_DEV
        ids = owners * IDX_DEV + slots
        shuffled = ids[jax.random.permutation(jax.random.fold_in(dkey, 3), pairs)]
        return shuffled.reshape(Q_DEV, K)
    return jax.vmap(one_device)(jnp.arange(devices)).reshape(QUERIES, K).astype(jnp.int32)


def level_of(own_key, shape, pieces, least, high):
    gain = 1.0
    for position, parts in pieces:
        steps = jax.random.uniform(jax.random.fold_in(jax.random.fold_in(own_key, 6), position), (parts,), jnp.float32, least / len(pieces), high / len(pieces))
        gain = gain * jnp.repeat(jnp.exp(steps), shape[position] // parts).reshape((-1,) + (1,) * (len(shape) - 1 - position))
    return gain


def bell_draw(own_key, extent, width, limit, split=(), kind=jnp.bfloat16):
    values = jax.random.normal(own_key, extent, jnp.float32) * width
    if len(split) > 0:
        values = level_of(own_key, extent, split, -0.22, 0.18) * values
    return jnp.clip(values, min=-limit, max=limit).astype(kind)


def setup_inputs(seed: int = 0) -> dict:
    arg_keys = jax.random.split(jax.random.key(seed), 7)
    queries = bell_draw(arg_keys[0], (QUERIES, F, R * REGION_FEATURES), 1.0, 6.0, ((0, 128),))
    index_videos = bell_draw(arg_keys[1], (VIDEOS, F, R * REGION_FEATURES), 1.0, 6.0, ((0, 128),))
    candidates = draw_candidates(jax.random.fold_in(arg_keys[6], 71), 0)
    conv_one = bell_draw(arg_keys[3], (C1, 1, 3, 3), 9 ** -0.5, 2.0)
    conv_two = bell_draw(arg_keys[4], (C2, C1, 3, 3), (9 * C1) ** -0.5, 0.375)
    conv_three = bell_draw(arg_keys[5], (1, C2, 3, 3), (9 * C2) ** -0.5, 0.25)
    return dict(queries=queries, index_videos=index_videos, candidates=candidates, conv_one=conv_one, conv_two=conv_two, conv_three=conv_three)


def conv_same(x, w):
    return lax.conv_general_dilated(x.astype(jnp.float32), w.astype(jnp.float32), (1, 1), 'SAME', dimension_numbers=('NCHW', 'OIHW', 'NCHW'))

def pool_two(x):
    b, c, h, w = x.shape
    return lax.optimization_barrier(jnp.max(x.reshape(b, c, h // 2, 2, w // 2, 2), axis=(3, 5)))

def pair_scores(left, right, conv_one, conv_two, conv_three):
    count = left.shape[0]
    left_frame_features = left.astype(jnp.float32).reshape(count, F * R, REGION_FEATURES)
    right_frame_features = right.astype(jnp.float32).reshape(count, F * R, REGION_FEATURES)
    region_similarities = jnp.einsum('avs,afs->avf', left_frame_features, right_frame_features) * (1.0 / math.sqrt(REGION_FEATURES))
    region_similarities = region_similarities.reshape(count, F, R, F, R)
    frame_map = lax.optimization_barrier(jnp.mean(lax.optimization_barrier(jnp.max(region_similarities, axis=4)), axis=2)).astype(jnp.bfloat16)
    first = pool_two(jax.nn.relu(conv_same(frame_map[:, None], conv_one))).astype(jnp.bfloat16)
    second = pool_two(jax.nn.relu(conv_same(first, conv_two))).astype(jnp.bfloat16)
    final = conv_same(second, conv_three)[:, 0]
    return lax.optimization_barrier(jnp.mean(lax.optimization_barrier(jnp.max(jnp.clip(final, -1.0, 1.0), axis=2)), axis=1))

def reference(queries, index_videos, candidates, conv_one, conv_two, conv_three):
    total = QUERIES * K
    flat = candidates.reshape(total)
    owner_query = (jnp.arange(total) // K).astype(jnp.int32)
    block = 64

    def one_block(i):
        start = (i * block).astype(jnp.int32)
        ids = lax.dynamic_slice_in_dim(flat, start, block)
        rows = lax.dynamic_slice_in_dim(owner_query, start, block)
        return pair_scores(queries[rows], index_videos[ids], conv_one, conv_two, conv_three)
    result = lax.map(one_block, jnp.arange(total // block, dtype=jnp.int32))
    return result.reshape(QUERIES, K)
```

```python
import functools
import math

import jax
import jax.numpy as jnp
from jax import lax
from jax.experimental import pallas as pl
from jax.experimental.pallas import tpu as pltpu
from jax.sharding import PartitionSpec as P

MESH = pl.DeviceIdType.MESH
F = 8
R = 5
REGION_FEATURES = 1920
WIDTH = R * REGION_FEATURES
THIRD = WIDTH // 3
SIDE = 4
Q_DEV = 16
K = 8
DEVICES = 128
IDX_DEV = 128
SLOTS = 2 * DEVICES
AXES = ((0, 1, 2), (1, 2, 0), (2, 0, 1))


def position():
    i = lax.axis_index("shard")
    return (i // 32, (i // 8) % 4, (i // 2) % 4), i % 2


def device_at(chip, core):
    return ((chip[0] % 4) * 4 + chip[1] % 4) * 8 + (chip[2] % 4) * 2 + core % 2


def shifted(chip, axis, step):
    moved = list(chip)
    moved[axis] = moved[axis] + step
    return tuple(moved)


def greet(peers):
    barrier = pltpu.get_barrier_semaphore()
    for peer in peers:
        pl.semaphore_signal(barrier, inc=1, device_id=(peer,), device_id_type=MESH)
    pl.semaphore_wait(barrier, len(peers))


def gather_kernel(q_ref, g_ref, send_sem, recv_sem, local_sem):
    chip, core = position()
    near = {
        (axis, step): device_at(shifted(chip, axis, step), core) for axis in range(3) for step in (1, -1)
    }
    half = Q_DEV // 2
    greet(list(near.values()))
    started = []
    arrivals = {}

    span = {0: pl.ds(0, Q_DEV), 1: pl.ds(0, half), 2: pl.ds(half, half)}

    def send(t, axis_place, step, da, db, to_a, to_b, piece):
        number = len(started)
        axis = AXES[t][axis_place]
        if (da, db) == (0, 0):
            source = q_ref.at[span[piece], :, pl.ds(t * THIRD, THIRD)]
        else:
            source = g_ref.at[t, da, db, span[piece]]
        copy = pltpu.make_async_remote_copy(
            src_ref=source,
            dst_ref=g_ref.at[t, to_a, to_b, span[piece]],
            send_sem=send_sem.at[number],
            recv_sem=recv_sem.at[number],
            device_id=(near[axis, step],),
            device_id_type=MESH,
        )
        copy.start()
        started.append(copy)
        arrivals[t, to_a, to_b, piece] = copy

    def have(t, a, b, piece=0):
        arrivals[t, a, b, piece].wait_recv()

    def out_b(t, da):
        send(t, 1, 1, da, 0, da, 3, 0)
        send(t, 1, -1, da, 0, da, 1, 0)

    def on_b(t, da):
        have(t, da, 3)
        send(t, 1, 1, da, 3, da, 2, 1)
        have(t, da, 1)
        send(t, 1, -1, da, 1, da, 2, 2)

    thirds = range(3)
    for t in thirds:
        send(t, 0, 1, 0, 0, 3, 0, 0)
        send(t, 0, -1, 0, 0, 1, 0, 0)
    for t in thirds:
        out_b(t, 0)
    own = []
    for t in thirds:
        copy = pltpu.make_async_copy(
            q_ref.at[:, :, pl.ds(t * THIRD, THIRD)], g_ref.at[t, 0, 0], local_sem.at[t]
        )
        copy.start()
        own.append(copy)
    for t in thirds:
        have(t, 3, 0)
        send(t, 0, 1, 3, 0, 2, 0, 1)
        have(t, 1, 0)
        send(t, 0, -1, 1, 0, 2, 0, 2)
    for t in thirds:
        out_b(t, 3)
        out_b(t, 1)
    for t in thirds:
        on_b(t, 0)
    for t in thirds:
        have(t, 2, 0, 1)
        have(t, 2, 0, 2)
        out_b(t, 2)
    for da in (3, 1, 2):
        for t in thirds:
            on_b(t, da)
    for t in thirds:
        for da in range(4):
            have(t, da, 2, 1)
            have(t, da, 2, 2)
    for copy in started:
        copy.wait_send()
    for copy in own:
        copy.wait()


COPIES = 60
RING = 4


def exchange_kernel(
    sel_ref, g_ref, rows_ref, got_0, got_1, got_2, out, got_sem, send_sem, recv_sem
):
    got = (got_0, got_1, got_2)
    chip, core = position()
    peers = [device_at(chip, core + 1)]
    for axis in range(3):
        for step in (1, 2, 3):
            for other in (0, 1):
                peers.append(device_at(shifted(chip, axis, step), core + other))
    greet(peers)

    def fetch(block, t):
        return pltpu.make_async_copy(
            g_ref.at[t, block // 4, block % 4], got[t], got_sem.at[t]
        )

    def copies(block, t, slot):
        a, b, c = AXES[t]
        from_chip = shifted(shifted(chip, a, block // 4), b, block % 4)
        source = device_at(from_chip, core)
        made = []
        for step in range(4):
            for other in (0, 1):
                n = step * 2 + other
                src = out.at[slot, n]
                dst = rows_ref.at[source, :, :, pl.ds(t * THIRD, THIRD)]
                if n == 0:
                    made.append(pltpu.make_async_copy(src, dst, send_sem.at[slot, n]))
                else:
                    made.append(
                        pltpu.make_async_remote_copy(
                            src_ref=src,
                            dst_ref=dst,
                            send_sem=send_sem.at[slot, n],
                            recv_sem=recv_sem.at[t, block, n],
                            device_id=(device_at(shifted(chip, c, step), core + other),),
                            device_id_type=MESH,
                        )
                    )
        return made

    def drain(block, t, slot):
        for n, copy in enumerate(copies(block, t, slot)):
            if n == 0:
                copy.wait()
            else:
                copy.wait_send()

    for t in range(3):
        fetch(0, t).start()

    def one_block(block, carry):
        for t in range(3):
            slot = t * RING + block % RING

            @pl.when(block >= RING)
            def _():
                drain(block - RING, t, slot)

            fetch(block, t).wait()
            for n in range(8):
                for rank in range(2):
                    pick = sel_ref[((t * 16 + block) * 8 + n) * 2 + rank]
                    out[slot, n, rank] = got[t][pick]
            for copy in copies(block, t, slot):
                copy.start()

            @pl.when(block < 15)
            def _():
                fetch(block + 1, t).start()

        return carry

    lax.fori_loop(0, 16, one_block, 0)
    for t in range(3):
        for block in range(16 - RING, 16):
            drain(block, t, t * RING + block % RING)

    def settle(block, carry):
        for t in range(3):
            for copy in copies(block, t, 0)[1:]:
                copy.wait_recv()
        return carry

    lax.fori_loop(0, 16, settle, 0)


GROUP = 8


def frame_kernel(wanted_ref, rows_ref, videos_ref, map_ref):
    step = pl.program_id(0)

    def one_source(i, carry):
        for rank in range(2):
            want = wanted_ref[(step * GROUP + i) * 2 + rank]
            row = rows_ref[i, rank]
            video = videos_ref[want]
            left = jnp.concatenate(
                [row[:, r * REGION_FEATURES : (r + 1) * REGION_FEATURES] for r in range(R)], axis=0
            )
            right = jnp.concatenate(
                [video[:, r * REGION_FEATURES : (r + 1) * REGION_FEATURES] for r in range(R)], axis=0
            )
            sim = lax.dot_general(
                left, right, (((1,), (1,)), ((), ())), preferred_element_type=jnp.float32
            )
            best = sim[:, 0:F]
            for s in range(1, R):
                best = jnp.maximum(best, sim[:, s * F : (s + 1) * F])
            total = best[0:F]
            for r in range(1, R):
                total = total + best[r * F : (r + 1) * F]
            map_ref[i, rank] = total * (1.0 / (math.sqrt(REGION_FEATURES) * R))
        return carry

    lax.fori_loop(0, GROUP, one_source, 0)


def conv_same(x, w):
    return lax.conv_general_dilated(
        x, w, (1, 1), "SAME", dimension_numbers=("NCHW", "OIHW", "NCHW"), preferred_element_type=jnp.float32
    )


def pool_two(x):
    b, c, h, w = x.shape
    return jnp.max(x.reshape(b, c, h // 2, 2, w // 2, 2), axis=(3, 5))


def body(queries, index_videos, candidates, conv_one, conv_two, conv_three):
    chip, core = position()
    me = lax.axis_index("shard")
    pairs = Q_DEV * K

    gathered = pl.pallas_call(
        gather_kernel,
        out_shape=jax.ShapeDtypeStruct((3, SIDE, SIDE, Q_DEV, F, THIRD), jnp.bfloat16),
        in_specs=[pl.BlockSpec(memory_space=pl.ANY)],
        out_specs=pl.BlockSpec(memory_space=pl.ANY),
        scratch_shapes=[
            pltpu.SemaphoreType.DMA((COPIES,)),
            pltpu.SemaphoreType.DMA((COPIES,)),
            pltpu.SemaphoreType.DMA((3,)),
        ],
        compiler_params=pltpu.CompilerParams(collective_id=0, has_side_effects=True),
        name="gather",
    )(queries)

    flat = candidates.reshape(pairs)
    everyone = lax.all_gather(flat, "shard")
    holder = everyone // IDX_DEV
    local = everyone % IDX_DEV
    order = lax.broadcasted_iota(jnp.int32, (DEVICES, pairs), 1)
    mine = holder == me
    key = order * IDX_DEV + local
    low = jnp.min(jnp.where(mine, key, pairs * IDX_DEV), axis=1)
    high = jnp.max(jnp.where(mine, key, 0), axis=1)
    wanted = jnp.stack([low % IDX_DEV, high % IDX_DEV], axis=1).reshape(SLOTS)

    offset = jnp.arange(16, dtype=jnp.int32)
    sources, targets = [], []
    for a, b, c in AXES:
        sources.append(device_at(shifted(shifted(chip, a, offset // 4), b, offset % 4), core))
        line = jnp.arange(8, dtype=jnp.int32)
        targets.append(device_at(shifted(chip, c, line // 2), core + line % 2))
    sources = jnp.stack(sources)
    targets = jnp.stack(targets)
    asked = holder[sources]
    hit = asked[:, :, None, :] == targets[:, None, :, None]
    query_of = lax.broadcasted_iota(jnp.int32, (1, 1, 1, pairs), 3) // K
    first_pick = jnp.min(jnp.where(hit, query_of, Q_DEV - 1), axis=3)
    last_pick = jnp.max(jnp.where(hit, query_of, 0), axis=3)
    sel = jnp.stack([first_pick, last_pick], axis=3).reshape(3 * 16 * 8 * 2)

    rows = pl.pallas_call(
        exchange_kernel,
        out_shape=jax.ShapeDtypeStruct((DEVICES, 2, F, WIDTH), jnp.bfloat16),
        in_specs=[pl.BlockSpec(memory_space=pltpu.SMEM), pl.BlockSpec(memory_space=pl.ANY)],
        out_specs=pl.BlockSpec(memory_space=pl.ANY),
        scratch_shapes=[
            pltpu.VMEM((Q_DEV, F, THIRD), jnp.bfloat16),
            pltpu.VMEM((Q_DEV, F, THIRD), jnp.bfloat16),
            pltpu.VMEM((Q_DEV, F, THIRD), jnp.bfloat16),
            pltpu.VMEM((3 * RING, 8, 2, F, THIRD), jnp.bfloat16),
            pltpu.SemaphoreType.DMA((3,)),
            pltpu.SemaphoreType.DMA((3 * RING, 8)),
            pltpu.SemaphoreType.DMA((3, 16, 8)),
        ],
        compiler_params=pltpu.CompilerParams(
            collective_id=1, has_side_effects=True, vmem_limit_bytes=40 << 20
        ),
        name="exchange",
    )(sel, gathered)

    maps = pl.pallas_call(
        frame_kernel,
        out_shape=jax.ShapeDtypeStruct((DEVICES, 2, F, F), jnp.float32),
        grid_spec=pltpu.PrefetchScalarGridSpec(
            num_scalar_prefetch=1,
            grid=(DEVICES // GROUP,),
            in_specs=[
                pl.BlockSpec((GROUP, 2, F, WIDTH), lambda i, w: (i, 0, 0, 0)),
                pl.BlockSpec((IDX_DEV, F, WIDTH), lambda i, w: (0, 0, 0), pipeline_mode=pl.Buffered(1)),
            ],
            out_specs=pl.BlockSpec((GROUP, 2, F, F), lambda i, w: (i, 0, 0, 0)),
        ),
        compiler_params=pltpu.CompilerParams(vmem_limit_bytes=48 << 20),
        name="frames",
    )(wanted, rows, index_videos)

    frame_map = maps.reshape(SLOTS, 1, F, F).astype(jnp.bfloat16)
    first = pool_two(jax.nn.relu(conv_same(frame_map, conv_one))).astype(jnp.bfloat16)
    second = pool_two(jax.nn.relu(conv_same(first, conv_two))).astype(jnp.bfloat16)
    final = conv_same(second, conv_three)[:, 0]
    scores = jnp.mean(jnp.max(jnp.clip(final, -1.0, 1.0), axis=2), axis=1)

    back = lax.all_to_all(scores.reshape(DEVICES, 2), "shard", split_axis=0, concat_axis=0, tiled=True)
    my_holder = flat // IDX_DEV
    same = my_holder[:, None] == my_holder[None, :]
    earlier = jnp.arange(pairs)[None, :] < jnp.arange(pairs)[:, None]
    second_one = jnp.any(same & earlier, axis=1)
    to_me = my_holder[:, None] == jnp.arange(DEVICES)[None, :]
    score_first = jnp.sum(jnp.where(to_me, back[None, :, 0], 0.0), axis=1)
    score_last = jnp.sum(jnp.where(to_me, back[None, :, 1], 0.0), axis=1)
    return jnp.where(second_one, score_last, score_first).reshape(Q_DEV, K)


def solution(mesh):
    placed = (P("shard", None, None), P("shard", None, None), P("shard", None), P(), P(), P())
    return jax.shard_map(
        body, mesh=mesh, in_specs=placed, out_specs=P("shard", None), check_vma=False
    )
```

```python
import functools
import math

import jax
import jax.numpy as jnp
from jax import lax
from jax.experimental import pallas as pl
from jax.experimental.pallas import tpu as pltpu
from jax.sharding import PartitionSpec as P

MESH = pl.DeviceIdType.MESH
F = 8
R = 5
REGION_FEATURES = 1920
WIDTH = R * REGION_FEATURES
THIRD = WIDTH // 3
PART = REGION_FEATURES // 3
SIDE = 4
Q_DEV = 16
K = 8
DEVICES = 128
IDX_DEV = 128
SLOTS = 2 * DEVICES
AXES = ((0, 1, 2), (1, 2, 0), (2, 0, 1))


def position():
    i = lax.axis_index("shard")
    return (i // 32, (i // 8) % 4, (i // 2) % 4), i % 2


def device_at(chip, core):
    return ((chip[0] % 4) * 4 + chip[1] % 4) * 8 + (chip[2] % 4) * 2 + core % 2


def shifted(chip, axis, step):
    moved = list(chip)
    moved[axis] = moved[axis] + step
    return tuple(moved)


def greet(peers):
    barrier = pltpu.get_barrier_semaphore()
    for peer in peers:
        pl.semaphore_signal(barrier, inc=1, device_id=(peer,), device_id_type=MESH)
    pl.semaphore_wait(barrier, len(peers))


def gather_kernel(q_ref, ids_ref, g_ref, table_ref, send_sem, recv_sem, local_sem, id_send, id_recv):
    chip, core = position()
    near = {
        (axis, step): device_at(shifted(chip, axis, step), core) for axis in range(3) for step in (1, 2, 3)
    }
    sibling = device_at(chip, core + 1)
    half = Q_DEV // 2
    own = []
    for t in range(3):
        for r in range(R):
            copy = pltpu.make_async_copy(
                q_ref.at[:, :, pl.ds(r * REGION_FEATURES + t * PART, PART)],
                g_ref.at[t, 0, 0, :, :, pl.ds(r * PART, PART)],
                local_sem.at[t, r],
            )
            own.append(copy)
    me = device_at(chip, core)
    own_ids = pltpu.make_async_copy(ids_ref, table_ref.at[pl.ds(me, 1)], local_sem.at[3, 0])
    own_ids.start()
    greet(list(near.values()) + [sibling])
    started = []
    arrivals = {}

    span = {0: pl.ds(0, Q_DEV), 1: pl.ds(0, half), 2: pl.ds(half, half)}

    def send_own(t, axis_place, step, to_a, to_b):
        axis = AXES[t][axis_place]
        for r in range(R):
            number = len(started)
            copy = pltpu.make_async_remote_copy(
                src_ref=q_ref.at[:, :, pl.ds(r * REGION_FEATURES + t * PART, PART)],
                dst_ref=g_ref.at[t, to_a, to_b, :, :, pl.ds(r * PART, PART)],
                send_sem=send_sem.at[number],
                recv_sem=recv_sem.at[number],
                device_id=(near[axis, step],),
                device_id_type=MESH,
            )
            copy.start()
            started.append(copy)
            arrivals[t, to_a, to_b, 3 + r] = copy

    def send(t, axis_place, step, da, db, to_a, to_b, piece):
        number = len(started)
        axis = AXES[t][axis_place]
        copy = pltpu.make_async_remote_copy(
            src_ref=g_ref.at[t, da, db, span[piece]],
            dst_ref=g_ref.at[t, to_a, to_b, span[piece]],
            send_sem=send_sem.at[number],
            recv_sem=recv_sem.at[number],
            device_id=(near[axis, step],),
            device_id_type=MESH,
        )
        copy.start()
        started.append(copy)
        arrivals[t, to_a, to_b, piece] = copy

    def have(t, a, b, piece=0):
        if (t, a, b, piece) in arrivals:
            arrivals[t, a, b, piece].wait_recv()
        else:
            for r in range(R):
                arrivals[t, a, b, 3 + r].wait_recv()

    def out_b(t, da):
        if da == 0:
            send_own(t, 1, 1, 0, 3)
            send_own(t, 1, 3, 0, 1)
        else:
            send(t, 1, 1, da, 0, da, 3, 0)
            send(t, 1, 3, da, 0, da, 1, 0)

    def on_b(t, da):
        have(t, da, 3)
        send(t, 1, 1, da, 3, da, 2, 1)
        have(t, da, 1)
        send(t, 1, 3, da, 1, da, 2, 2)

    id_copies = []

    def send_ids(first, count, peers):
        made = []
        for peer in peers:
            number = len(id_copies)
            copy = pltpu.make_async_remote_copy(
                src_ref=table_ref.at[pl.ds(first, count)],
                dst_ref=table_ref.at[pl.ds(first, count)],
                send_sem=id_send.at[number],
                recv_sem=id_recv.at[number],
                device_id=(peer,),
                device_id_type=MESH,
            )
            copy.start()
            made.append(copy)
            id_copies.append(copy)
        return made

    def line(axis):
        return [near[axis, step] for step in (1, 2, 3)]

    thirds = range(3)
    own_ids.wait()
    wave = send_ids(me, 1, [sibling])
    for t in thirds:
        send_own(t, 0, 1, 3, 0)
        send_own(t, 0, 3, 1, 0)
    for copy in wave:
        copy.wait_recv()
    wave = send_ids(me - core, 2, line(2))
    for t in thirds:
        out_b(t, 0)
    for copy in own:
        copy.start()
    for t in thirds:
        have(t, 3, 0)
        send(t, 0, 1, 3, 0, 2, 0, 1)
        have(t, 1, 0)
        send(t, 0, 3, 1, 0, 2, 0, 2)
    for t in thirds:
        out_b(t, 3)
        out_b(t, 1)
    for t in thirds:
        on_b(t, 0)
    for copy in wave:
        copy.wait_recv()
    wave = send_ids((me // 8) * 8, 8, line(1))
    for t in thirds:
        have(t, 2, 0, 1)
        have(t, 2, 0, 2)
        out_b(t, 2)
    for t in thirds:
        on_b(t, 3)
    for copy in wave:
        copy.wait_recv()
    wave = send_ids((me // 32) * 32, 32, line(0))
    for da in (1, 2):
        for t in thirds:
            on_b(t, da)
    for t in thirds:
        for da in range(4):
            have(t, da, 2, 1)
            have(t, da, 2, 2)
    for copy in wave:
        copy.wait_recv()
    for copy in started + id_copies:
        copy.wait_send()
    for copy in own:
        copy.wait()


COPIES = 108
RING = 4
LAG = 3
BLOCKS = SIDE * SIDE


def score_kernel(
    sel_ref, wanted_ref, g_ref, videos_ref, rows_ref, map_ref,
    got_0, got_1, got_2, out, row, videos, sims,
    got_sem, send_sem, recv_sem, self_sem, row_sem, video_sem,
):
    got = (got_0, got_1, got_2)
    chip, core = position()
    load_videos = pltpu.make_async_copy(videos_ref, videos, video_sem)
    load_videos.start()
    peers = [device_at(chip, core + 1)]
    for axis in range(3):
        for step in (1, 2, 3):
            for other in (0, 1):
                peers.append(device_at(shifted(chip, axis, step), core + other))
    greet(peers)

    def fetch(block, t):
        return pltpu.make_async_copy(
            g_ref.at[t, block // 4, block % 4], got[t], got_sem.at[t]
        )

    def copies(block, t):
        slot = t * RING + block % RING
        made = []
        for step in range(4):
            for other in (0, 1):
                n = step * 2 + other
                if n > 0:
                    made.append(
                        pltpu.make_async_remote_copy(
                            src_ref=out.at[slot, n],
                            dst_ref=rows_ref.at[t, block, n],
                            send_sem=send_sem.at[slot, n],
                            recv_sem=recv_sem.at[t, block, n],
                            device_id=(device_at(shifted(chip, AXES[t][2], step), core + other),),
                            device_id_type=MESH,
                        )
                    )
        return made

    def keep(block, t):
        slot = t * RING + block % RING
        return pltpu.make_async_copy(out.at[slot, 0], rows_ref.at[t, block, 0], self_sem.at[slot])

    def load_row(block, t):
        return pltpu.make_async_copy(rows_ref.at[t, block], row.at[t], row_sem.at[t])

    def drain(block, t):
        for copy in copies(block, t):
            copy.wait_send()

    for t in range(3):
        fetch(0, t).start()

    def pack(block, t):
        @pl.when(block >= RING)
        def _():
            drain(block - RING, t)

        fetch(block, t).wait()
        slot = t * RING + block % RING
        for n in range(8):
            for rank in range(2):
                pick = sel_ref[((t * BLOCKS + block) * 8 + n) * 2 + rank]
                out[slot, n, rank] = got[t][pick]
        for copy in copies(block, t):
            copy.start()
        keep(block, t).start()

        @pl.when(block < BLOCKS - 1)
        def _():
            fetch(block + 1, t).start()

    def receive(block, t):
        for copy in copies(block, t):
            copy.wait_recv()
        keep(block, t).wait()
        load_row(block, t).start()

    def add_up(block, t):
        load_row(block, t).wait()
        a, b, c = AXES[t]
        from_line = shifted(shifted(chip, a, block // 4), b, block % 4)

        def one(n, carry):
            source = device_at(shifted(from_line, c, 4 - n // 2), core + n % 2)
            for rank in range(2):
                at = source * 2 + rank
                want = wanted_ref[at]
                left = jnp.concatenate(
                    [row[t, n, rank, :, r * PART : (r + 1) * PART] for r in range(R)], axis=0
                )
                right = jnp.concatenate(
                    [
                        videos[want, :, pl.ds(s * REGION_FEATURES + t * PART, PART)]
                        for s in range(R)
                    ],
                    axis=0,
                )
                sims[at] += lax.dot_general(
                    left, right, (((1,), (1,)), ((), ())), preferred_element_type=jnp.float32
                )
            return carry

        lax.fori_loop(0, 8, one, 0)

    def one_block(block, carry):
        @pl.when(block == LAG)
        def _():
            sims[...] = jnp.zeros_like(sims)
            load_videos.wait()

        for t in range(3):
            @pl.when(block < BLOCKS)
            def _():
                pack(block, t)

            @pl.when(jnp.logical_and(block > LAG, block <= BLOCKS + LAG))
            def _():
                add_up(block - LAG - 1, t)

            @pl.when(jnp.logical_and(block >= LAG, block < BLOCKS + LAG))
            def _():
                receive(block - LAG, t)

        return carry

    lax.fori_loop(0, BLOCKS + LAG + 1, one_block, 0)
    for t in range(3):
        for block in range(BLOCKS - RING, BLOCKS):
            drain(block, t)

    def finish(at, carry):
        sim = sims[at]
        best = sim[:, 0:F]
        for s in range(1, R):
            best = jnp.maximum(best, sim[:, s * F : (s + 1) * F])
        total = best[0:F]
        for r in range(1, R):
            total = total + best[r * F : (r + 1) * F]
        map_ref[at] = total * (1.0 / (math.sqrt(REGION_FEATURES) * R))
        return carry

    lax.fori_loop(0, SLOTS, finish, 0, unroll=4)


def conv_same(x, w):
    return lax.conv_general_dilated(
        x, w, (1, 1), "SAME", dimension_numbers=("NCHW", "OIHW", "NCHW"), preferred_element_type=jnp.float32
    )


def pool_two(x):
    b, c, h, w = x.shape
    return jnp.max(x.reshape(b, c, h // 2, 2, w // 2, 2), axis=(3, 5))


def body(queries, index_videos, candidates, conv_one, conv_two, conv_three):
    chip, core = position()
    me = lax.axis_index("shard")
    pairs = Q_DEV * K

    flat = candidates.reshape(pairs)
    gathered, everyone = pl.pallas_call(
        gather_kernel,
        out_shape=(
            jax.ShapeDtypeStruct((3, SIDE, SIDE, Q_DEV, F, THIRD), jnp.bfloat16),
            jax.ShapeDtypeStruct((DEVICES, 1, pairs), jnp.int32),
        ),
        in_specs=[pl.BlockSpec(memory_space=pl.ANY)] * 2,
        out_specs=(pl.BlockSpec(memory_space=pl.ANY), pl.BlockSpec(memory_space=pl.ANY)),
        scratch_shapes=[
            pltpu.SemaphoreType.DMA((COPIES,)),
            pltpu.SemaphoreType.DMA((COPIES,)),
            pltpu.SemaphoreType.DMA((4, R)),
            pltpu.SemaphoreType.DMA((10,)),
            pltpu.SemaphoreType.DMA((10,)),
        ],
        compiler_params=pltpu.CompilerParams(collective_id=0, has_side_effects=True),
        name="gather",
    )(queries, flat.reshape(1, 1, pairs))
    everyone = everyone.reshape(DEVICES, pairs)
    holder = everyone // IDX_DEV
    local = everyone % IDX_DEV
    order = lax.broadcasted_iota(jnp.int32, (DEVICES, pairs), 1)
    mine = holder == me
    key = order * IDX_DEV + local
    low = jnp.min(jnp.where(mine, key, pairs * IDX_DEV), axis=1)
    high = jnp.max(jnp.where(mine, key, 0), axis=1)
    wanted = jnp.stack([low % IDX_DEV, high % IDX_DEV], axis=1).reshape(SLOTS)

    offset = jnp.arange(16, dtype=jnp.int32)
    sources, targets = [], []
    for a, b, c in AXES:
        sources.append(device_at(shifted(shifted(chip, a, offset // 4), b, offset % 4), core))
        line = jnp.arange(8, dtype=jnp.int32)
        targets.append(device_at(shifted(chip, c, line // 2), core + line % 2))
    sources = jnp.stack(sources)
    targets = jnp.stack(targets)
    asked = holder[sources]
    hit = asked[:, :, None, :] == targets[:, None, :, None]
    query_of = lax.broadcasted_iota(jnp.int32, (1, 1, 1, pairs), 3) // K
    first_pick = jnp.min(jnp.where(hit, query_of, Q_DEV - 1), axis=3)
    last_pick = jnp.max(jnp.where(hit, query_of, 0), axis=3)
    sel = jnp.stack([first_pick, last_pick], axis=3).reshape(3 * 16 * 8 * 2)

    _, maps = pl.pallas_call(
        score_kernel,
        out_shape=(
            jax.ShapeDtypeStruct((3, BLOCKS, 8, 2, F, THIRD), jnp.bfloat16),
            jax.ShapeDtypeStruct((SLOTS, F, F), jnp.float32),
        ),
        in_specs=[
            pl.BlockSpec(memory_space=pltpu.SMEM),
            pl.BlockSpec(memory_space=pltpu.SMEM),
            pl.BlockSpec(memory_space=pl.ANY),
            pl.BlockSpec(memory_space=pl.ANY),
        ],
        out_specs=(
            pl.BlockSpec(memory_space=pl.ANY),
            pl.BlockSpec(memory_space=pltpu.VMEM),
        ),
        scratch_shapes=[
            pltpu.VMEM((Q_DEV, F, THIRD), jnp.bfloat16),
            pltpu.VMEM((Q_DEV, F, THIRD), jnp.bfloat16),
            pltpu.VMEM((Q_DEV, F, THIRD), jnp.bfloat16),
            pltpu.VMEM((3 * RING, 8, 2, F, THIRD), jnp.bfloat16),
            pltpu.VMEM((3, 8, 2, F, THIRD), jnp.bfloat16),
            pltpu.VMEM((IDX_DEV, F, WIDTH), jnp.bfloat16),
            pltpu.VMEM((SLOTS, F * R, F * R), jnp.float32),
            pltpu.SemaphoreType.DMA((3,)),
            pltpu.SemaphoreType.DMA((3 * RING, 8)),
            pltpu.SemaphoreType.DMA((3, BLOCKS, 8)),
            pltpu.SemaphoreType.DMA((3 * RING,)),
            pltpu.SemaphoreType.DMA((3,)),
            pltpu.SemaphoreType.DMA,
        ],
        compiler_params=pltpu.CompilerParams(
            collective_id=1, has_side_effects=True, vmem_limit_bytes=56 << 20
        ),
        name="score",
    )(sel, wanted, gathered, index_videos)

    frame_map = maps.reshape(SLOTS, 1, F, F).astype(jnp.bfloat16)
    first = pool_two(jax.nn.relu(conv_same(frame_map, conv_one))).astype(jnp.bfloat16)
    second = pool_two(jax.nn.relu(conv_same(first, conv_two))).astype(jnp.bfloat16)
    final = conv_same(second, conv_three)[:, 0]
    scores = jnp.mean(jnp.max(jnp.clip(final, -1.0, 1.0), axis=2), axis=1)

    back = lax.all_to_all(scores.reshape(DEVICES, 2), "shard", split_axis=0, concat_axis=0, tiled=True)
    my_holder = flat // IDX_DEV
    same = my_holder[:, None] == my_holder[None, :]
    earlier = jnp.arange(pairs)[None, :] < jnp.arange(pairs)[:, None]
    second_one = jnp.any(same & earlier, axis=1)
    to_me = my_holder[:, None] == jnp.arange(DEVICES)[None, :]
    score_first = jnp.sum(jnp.where(to_me, back[None, :, 0], 0.0), axis=1)
    score_last = jnp.sum(jnp.where(to_me, back[None, :, 1], 0.0), axis=1)
    return jnp.where(second_one, score_last, score_first).reshape(Q_DEV, K)


def solution(mesh):
    placed = (P("shard", None, None), P("shard", None, None), P("shard", None), P(), P(), P())
    return jax.shard_map(
        body, mesh=mesh, in_specs=placed, out_specs=P("shard", None), check_vma=False
    )
```

```python
import functools
import math

import jax
import jax.numpy as jnp
from jax import lax
from jax.experimental import pallas as pl
from jax.experimental.pallas import tpu as pltpu
from jax.sharding import PartitionSpec as P

MESH = pl.DeviceIdType.MESH
F = 8
R = 5
REGION_FEATURES = 1920
WIDTH = R * REGION_FEATURES
THIRD = WIDTH // 3
PART = REGION_FEATURES // 3
SIDE = 4
Q_DEV = 16
K = 8
DEVICES = 128
IDX_DEV = 128
SLOTS = 2 * DEVICES
AXES = ((0, 1, 2), (1, 2, 0), (2, 0, 1))


def position():
    i = lax.axis_index("shard")
    return (i // 32, (i // 8) % 4, (i // 2) % 4), i % 2


def device_at(chip, core):
    return ((chip[0] % 4) * 4 + chip[1] % 4) * 8 + (chip[2] % 4) * 2 + core % 2


def shifted(chip, axis, step):
    moved = list(chip)
    moved[axis] = moved[axis] + step
    return tuple(moved)


def greet(peers):
    barrier = pltpu.get_barrier_semaphore()
    for peer in peers:
        pl.semaphore_signal(barrier, inc=1, device_id=(peer,), device_id_type=MESH)
    pl.semaphore_wait(barrier, len(peers))


def gather(chip, core, q_ref, ids_ref, g_ref, table_ref, make_tables, send_sem, recv_sem, local_sem, id_send, id_recv):
    near = {
        (axis, step): device_at(shifted(chip, axis, step), core) for axis in range(3) for step in (1, 2, 3)
    }
    sibling = device_at(chip, core + 1)
    half = Q_DEV // 2
    own = []
    for t in range(3):
        for r in range(R):
            copy = pltpu.make_async_copy(
                q_ref.at[:, :, pl.ds(r * REGION_FEATURES + t * PART, PART)],
                g_ref.at[t, 0, 0, :, :, pl.ds(r * PART, PART)],
                local_sem.at[t, r],
            )
            own.append(copy)
    me = device_at(chip, core)
    own_ids = pltpu.make_async_copy(ids_ref, table_ref.at[pl.ds(me, 1)], local_sem.at[3, 0])
    own_ids.start()
    started = []
    arrivals = {}

    span = {0: pl.ds(0, Q_DEV), 1: pl.ds(0, half), 2: pl.ds(half, half)}

    def send_own(t, axis_place, step, to_a, to_b):
        axis = AXES[t][axis_place]
        for r in range(R):
            number = len(started)
            copy = pltpu.make_async_remote_copy(
                src_ref=q_ref.at[:, :, pl.ds(r * REGION_FEATURES + t * PART, PART)],
                dst_ref=g_ref.at[t, to_a, to_b, :, :, pl.ds(r * PART, PART)],
                send_sem=send_sem.at[number],
                recv_sem=recv_sem.at[number],
                device_id=(near[axis, step],),
                device_id_type=MESH,
            )
            copy.start()
            started.append(copy)
            arrivals[t, to_a, to_b, 3 + r] = copy

    def send(t, axis_place, step, da, db, to_a, to_b, piece):
        number = len(started)
        axis = AXES[t][axis_place]
        copy = pltpu.make_async_remote_copy(
            src_ref=g_ref.at[t, da, db, span[piece]],
            dst_ref=g_ref.at[t, to_a, to_b, span[piece]],
            send_sem=send_sem.at[number],
            recv_sem=recv_sem.at[number],
            device_id=(near[axis, step],),
            device_id_type=MESH,
        )
        copy.start()
        started.append(copy)
        arrivals[t, to_a, to_b, piece] = copy

    def have(t, a, b, piece=0):
        if (t, a, b, piece) in arrivals:
            arrivals[t, a, b, piece].wait_recv()
        else:
            for r in range(R):
                arrivals[t, a, b, 3 + r].wait_recv()

    def out_b(t, da):
        if da == 0:
            send_own(t, 1, 1, 0, 3)
            send_own(t, 1, 3, 0, 1)
        else:
            send(t, 1, 1, da, 0, da, 3, 0)
            send(t, 1, 3, da, 0, da, 1, 0)

    def on_b(t, da):
        have(t, da, 3)
        send(t, 1, 1, da, 3, da, 2, 1)
        have(t, da, 1)
        send(t, 1, 3, da, 1, da, 2, 2)

    id_copies = []

    def send_ids(first, count, peers):
        made = []
        for peer in peers:
            number = len(id_copies)
            copy = pltpu.make_async_remote_copy(
                src_ref=table_ref.at[pl.ds(first, count)],
                dst_ref=table_ref.at[pl.ds(first, count)],
                send_sem=id_send.at[number],
                recv_sem=id_recv.at[number],
                device_id=(peer,),
                device_id_type=MESH,
            )
            copy.start()
            made.append(copy)
            id_copies.append(copy)
        return made

    def line(axis):
        return [near[axis, step] for step in (1, 2, 3)]

    thirds = range(3)
    own_ids.wait()
    wave = send_ids(me, 1, [sibling])
    for t in thirds:
        send_own(t, 0, 1, 3, 0)
        send_own(t, 0, 3, 1, 0)
    for copy in wave:
        copy.wait_recv()
    wave = send_ids(me - core, 2, line(2))
    for t in thirds:
        out_b(t, 0)
    for copy in own:
        copy.start()
    for t in thirds:
        have(t, 3, 0)
        send(t, 0, 1, 3, 0, 2, 0, 1)
        have(t, 1, 0)
        send(t, 0, 3, 1, 0, 2, 0, 2)
    for t in thirds:
        out_b(t, 3)
        out_b(t, 1)
    for t in thirds:
        on_b(t, 0)
    for copy in wave:
        copy.wait_recv()
    wave = send_ids((me // 8) * 8, 8, line(1))
    for t in thirds:
        have(t, 2, 0, 1)
        have(t, 2, 0, 2)
        out_b(t, 2)
    for t in thirds:
        on_b(t, 3)
    for copy in wave:
        copy.wait_recv()
    wave = send_ids((me // 32) * 32, 32, line(0))
    for t in thirds:
        on_b(t, 1)
    for copy in wave:
        copy.wait_recv()
    make_tables()
    for t in thirds:
        on_b(t, 2)
    for copy in own:
        copy.wait()

    def the_rest():
        for t in thirds:
            for da in range(4):
                have(t, da, 2, 1)
                have(t, da, 2, 2)

    def all_sent():
        for copy in started + id_copies:
            copy.wait_send()

    return the_rest, all_sent


COPIES = 108
RING = 4
LAG = 3
BLOCKS = SIDE * SIDE


def order_of(da, db):
    far = db // 2 - db // 3
    return far * (12 + da) + (1 - far) * (da * 3 + db - db // 3)


def offsets_at(step):
    far = step // 12
    third = step % 3
    return (1 - far) * (step // 3) + far * (step - 12), (1 - far) * (third + third // 2) + far * 2


def score_kernel(
    q_ref, ids_ref, videos_ref, g_ref, rows_ref, map_ref,
    got_0, got_1, got_2, out, row, videos, sims, table, sel, wanted, sel_ref, wanted_ref,
    gather_send, gather_recv, local_sem, id_send, id_recv,
    got_sem, send_sem, recv_sem, self_sem, row_sem, video_sem, table_sem,
):
    got = (got_0, got_1, got_2)
    chip, core = position()
    me = device_at(chip, core)
    peers = [device_at(chip, core + 1)]
    for axis in range(3):
        for step in (1, 2, 3):
            for other in (0, 1):
                peers.append(device_at(shifted(chip, axis, step), core + other))
    load_videos = pltpu.make_async_copy(videos_ref, videos, video_sem)

    def make_tables():
        lane = lax.broadcasted_iota(jnp.int32, (1, Q_DEV * K), 1)
        lanes = lax.broadcasted_iota(jnp.int32, (8, Q_DEV * K), 1)
        places = lax.broadcasted_iota(jnp.int32, (8, Q_DEV * K), 0)

        def one_source(source, carry):
            ids = table[source]
            key = lane * IDX_DEV + ids % IDX_DEV
            mine = ids // IDX_DEV == me
            low = jnp.min(jnp.where(mine, key, Q_DEV * K * IDX_DEV), axis=1, keepdims=True)
            high = jnp.max(jnp.where(mine, key, 0), axis=1, keepdims=True)
            wanted[source] = jnp.where(lane == 0, low % IDX_DEV, high % IDX_DEV)
            return carry

        lax.fori_loop(0, DEVICES, one_source, 0, unroll=8)

        for t in range(3):
            a, b, c = AXES[t]
            spots = shifted(chip, c, places // 2)
            target = device_at(spots, core + places % 2)

            def one_block(step, carry):
                da, db = offsets_at(step)
                source = device_at(shifted(shifted(chip, a, da), b, db), core)
                hit = jnp.broadcast_to(table[source] // IDX_DEV, (8, Q_DEV * K)) == target
                first = jnp.min(jnp.where(hit, lanes // K, Q_DEV - 1), axis=1, keepdims=True)
                last = jnp.max(jnp.where(hit, lanes // K, 0), axis=1, keepdims=True)
                sel[t * BLOCKS + step] = jnp.where(lanes == 0, first, last)
                return carry

            lax.fori_loop(0, BLOCKS, one_block, 0, unroll=4)
        moves = [
            pltpu.make_async_copy(wanted, wanted_ref, table_sem.at[0]),
            pltpu.make_async_copy(sel, sel_ref, table_sem.at[1]),
        ]
        for move in moves:
            move.start()
        for move in moves:
            move.wait()

    greet(peers)
    the_rest, all_sent = gather(
        chip, core, q_ref, ids_ref, g_ref, table, make_tables,
        gather_send, gather_recv, local_sem, id_send, id_recv,
    )
    load_videos.start()

    def fetch(block, t):
        da, db = offsets_at(block)
        return pltpu.make_async_copy(g_ref.at[t, da, db], got[t], got_sem.at[t])

    def copies(block, t):
        slot = t * RING + block % RING
        made = []
        for step in range(4):
            for other in (0, 1):
                n = step * 2 + other
                if n > 0:
                    made.append(
                        pltpu.make_async_remote_copy(
                            src_ref=out.at[slot, n],
                            dst_ref=rows_ref.at[t, block, n],
                            send_sem=send_sem.at[slot, n],
                            recv_sem=recv_sem.at[t, block, n],
                            device_id=(device_at(shifted(chip, AXES[t][2], step), core + other),),
                            device_id_type=MESH,
                        )
                    )
        return made

    def keep(block, t):
        slot = t * RING + block % RING
        return pltpu.make_async_copy(out.at[slot, 0], rows_ref.at[t, block, 0], self_sem.at[slot])

    def load_row(block, t):
        return pltpu.make_async_copy(rows_ref.at[t, block], row.at[t], row_sem.at[t])

    def drain(block, t):
        for copy in copies(block, t):
            copy.wait_send()

    for t in range(3):
        fetch(0, t).start()

    def pack(block, t):
        @pl.when(block >= RING)
        def _():
            drain(block - RING, t)

        fetch(block, t).wait()
        slot = t * RING + block % RING
        for n in range(8):
            for rank in range(2):
                pick = sel_ref[t * BLOCKS + block, n, rank]
                out[slot, n, rank] = got[t][pick]
        for copy in copies(block, t):
            copy.start()
        keep(block, t).start()

        @pl.when(block < BLOCKS - 1)
        def _():
            fetch(block + 1, t).start()

    def receive(block, t):
        for copy in copies(block, t):
            copy.wait_recv()
        keep(block, t).wait()
        load_row(block, t).start()

    def finish(at):
        sim = sims[at]
        best = sim[:, 0:F]
        for s in range(1, R):
            best = jnp.maximum(best, sim[:, s * F : (s + 1) * F])
        total = best[0:F]
        for r in range(1, R):
            total = total + best[r * F : (r + 1) * F]
        map_ref[at] = total * (1.0 / (math.sqrt(REGION_FEATURES) * R))

    def add_up(block, t):
        load_row(block, t).wait()
        a, b, c = AXES[t]
        da, db = offsets_at(block)
        from_line = shifted(shifted(chip, a, da), b, db)

        def one(n, carry):
            dc = (4 - n // 2) % 4
            source = device_at(shifted(from_line, c, dc), core + n % 2)
            now = block * 3 + t
            next_one = order_of(db, dc) * 3 + (t + 1) % 3
            other_one = order_of(dc, da) * 3 + (t + 2) % 3
            for rank in range(2):
                at = source * 2 + rank
                want = wanted_ref[source, 0, rank]
                left = jnp.concatenate(
                    [row[t, n, rank, :, r * PART : (r + 1) * PART] for r in range(R)], axis=0
                )
                right = jnp.concatenate(
                    [
                        videos[want, :, pl.ds(s * REGION_FEATURES + t * PART, PART)]
                        for s in range(R)
                    ],
                    axis=0,
                )
                sims[at] += lax.dot_general(
                    left, right, (((1,), (1,)), ((), ())), preferred_element_type=jnp.float32
                )

            @pl.when(jnp.logical_and(now > next_one, now > other_one))
            def _():
                finish(source * 2)
                finish(source * 2 + 1)

            return carry

        lax.fori_loop(0, 8, one, 0, unroll=2)

    def one_block(block, carry):
        @pl.when(block == LAG)
        def _():
            sims[...] = jnp.zeros_like(sims)
            load_videos.wait()

        @pl.when(block == 11)
        def _():
            the_rest()

        for t in range(3):
            @pl.when(block < BLOCKS)
            def _():
                pack(block, t)

            @pl.when(jnp.logical_and(block > LAG, block <= BLOCKS + LAG))
            def _():
                add_up(block - LAG - 1, t)

            @pl.when(jnp.logical_and(block >= LAG, block < BLOCKS + LAG))
            def _():
                receive(block - LAG, t)

        return carry

    lax.fori_loop(0, BLOCKS + LAG + 1, one_block, 0)
    for t in range(3):
        for block in range(BLOCKS - RING, BLOCKS):
            drain(block, t)

    all_sent()


def conv_same(x, w):
    return lax.conv_general_dilated(
        x, w, (1, 1), "SAME", dimension_numbers=("NCHW", "OIHW", "NCHW"), preferred_element_type=jnp.float32
    )


def pool_two(x):
    b, c, h, w = x.shape
    return jnp.max(x.reshape(b, c, h // 2, 2, w // 2, 2), axis=(3, 5))


def body(queries, index_videos, candidates, conv_one, conv_two, conv_three):
    pairs = Q_DEV * K

    flat = candidates.reshape(pairs)
    _, _, maps = pl.pallas_call(
        score_kernel,
        out_shape=(
            jax.ShapeDtypeStruct((3, SIDE, SIDE, Q_DEV, F, THIRD), jnp.bfloat16),
            jax.ShapeDtypeStruct((3, BLOCKS, 8, 2, F, THIRD), jnp.bfloat16),
            jax.ShapeDtypeStruct((SLOTS, F, F), jnp.float32),
        ),
        in_specs=[pl.BlockSpec(memory_space=pl.ANY)] * 3,
        out_specs=(
            pl.BlockSpec(memory_space=pl.ANY),
            pl.BlockSpec(memory_space=pl.ANY),
            pl.BlockSpec(memory_space=pltpu.VMEM),
        ),
        scratch_shapes=[
            pltpu.VMEM((Q_DEV, F, THIRD), jnp.bfloat16),
            pltpu.VMEM((Q_DEV, F, THIRD), jnp.bfloat16),
            pltpu.VMEM((Q_DEV, F, THIRD), jnp.bfloat16),
            pltpu.VMEM((3 * RING, 8, 2, F, THIRD), jnp.bfloat16),
            pltpu.VMEM((3, 8, 2, F, THIRD), jnp.bfloat16),
            pltpu.VMEM((IDX_DEV, F, WIDTH), jnp.bfloat16),
            pltpu.VMEM((SLOTS, F * R, F * R), jnp.float32),
            pltpu.VMEM((DEVICES, 1, pairs), jnp.int32),
            pltpu.VMEM((3 * BLOCKS, 8, pairs), jnp.int32),
            pltpu.VMEM((DEVICES, 1, pairs), jnp.int32),
            pltpu.SMEM((3 * BLOCKS, 8, pairs), jnp.int32),
            pltpu.SMEM((DEVICES, 1, pairs), jnp.int32),
            pltpu.SemaphoreType.DMA((COPIES,)),
            pltpu.SemaphoreType.DMA((COPIES,)),
            pltpu.SemaphoreType.DMA((4, R)),
            pltpu.SemaphoreType.DMA((10,)),
            pltpu.SemaphoreType.DMA((10,)),
            pltpu.SemaphoreType.DMA((3,)),
            pltpu.SemaphoreType.DMA((3 * RING, 8)),
            pltpu.SemaphoreType.DMA((3, BLOCKS, 8)),
            pltpu.SemaphoreType.DMA((3 * RING,)),
            pltpu.SemaphoreType.DMA((3,)),
            pltpu.SemaphoreType.DMA,
            pltpu.SemaphoreType.DMA((2,)),
        ],
        compiler_params=pltpu.CompilerParams(
            collective_id=0, has_side_effects=True, vmem_limit_bytes=56 << 20
        ),
        name="score",
    )(queries, flat.reshape(1, 1, pairs), index_videos)

    frame_map = maps.reshape(SLOTS, 1, F, F).astype(jnp.bfloat16)
    first = pool_two(jax.nn.relu(conv_same(frame_map, conv_one))).astype(jnp.bfloat16)
    second = pool_two(jax.nn.relu(conv_same(first, conv_two))).astype(jnp.bfloat16)
    final = conv_same(second, conv_three)[:, 0]
    scores = jnp.mean(jnp.max(jnp.clip(final, -1.0, 1.0), axis=2), axis=1)

    back = lax.all_to_all(scores.reshape(DEVICES, 2), "shard", split_axis=0, concat_axis=0, tiled=True)
    my_holder = flat // IDX_DEV
    same = my_holder[:, None] == my_holder[None, :]
    earlier = jnp.arange(pairs)[None, :] < jnp.arange(pairs)[:, None]
    second_one = jnp.any(same & earlier, axis=1)
    to_me = my_holder[:, None] == jnp.arange(DEVICES)[None, :]
    score_first = jnp.sum(jnp.where(to_me, back[None, :, 0], 0.0), axis=1)
    score_last = jnp.sum(jnp.where(to_me, back[None, :, 1], 0.0), axis=1)
    return jnp.where(second_one, score_last, score_first).reshape(Q_DEV, K)


def solution(mesh):
    placed = (P("shard", None, None), P("shard", None, None), P("shard", None), P(), P(), P())
    return jax.shard_map(
        body, mesh=mesh, in_specs=placed, out_specs=P("shard", None), check_vma=False
    )
```

```python
import functools
import math

import jax
import jax.numpy as jnp
from jax import lax
from jax.experimental import pallas as pl
from jax.experimental.pallas import tpu as pltpu
from jax.sharding import PartitionSpec as P

MESH = pl.DeviceIdType.MESH
F = 8
R = 5
REGION_FEATURES = 1920
WIDTH = R * REGION_FEATURES
PART = REGION_FEATURES // 3
FR = F * R
SIDE = 4
Q_DEV = 16
K = 8
DEVICES = 128
IDX_DEV = 128
SLOTS = 2 * DEVICES
AXES = ((0, 1, 2), (1, 2, 0), (2, 0, 1))


def position():
    i = lax.axis_index("shard")
    return (i // 32, (i // 8) % 4, (i // 2) % 4), i % 2


def device_at(chip, core):
    return ((chip[0] % 4) * 4 + chip[1] % 4) * 8 + (chip[2] % 4) * 2 + core % 2


def shifted(chip, axis, step):
    moved = list(chip)
    moved[axis] = moved[axis] + step
    return tuple(moved)


def greet(peers):
    barrier = pltpu.get_barrier_semaphore()
    for peer in peers:
        pl.semaphore_signal(barrier, inc=1, device_id=(peer,), device_id_type=MESH)
    pl.semaphore_wait(barrier, len(peers))


def gather(chip, core, q_ref, ids_ref, g_ref, table_ref, make_tables, send_sem, recv_sem, local_sem, id_send, id_recv):
    near = {
        (axis, step): device_at(shifted(chip, axis, step), core) for axis in range(3) for step in (1, 2, 3)
    }
    sibling = device_at(chip, core + 1)
    half = Q_DEV // 2
    own = []
    for t in range(3):
        for r in range(R):
            copy = pltpu.make_async_copy(
                q_ref.at[:, :, pl.ds(r * REGION_FEATURES + t * PART, PART)],
                g_ref.at[t, 0, 0, :, pl.ds(r * F, F)],
                local_sem.at[t, r],
            )
            own.append(copy)
    me = device_at(chip, core)
    own_ids = pltpu.make_async_copy(ids_ref, table_ref.at[pl.ds(me, 1)], local_sem.at[3, 0])
    own_ids.start()
    started = []
    arrivals = {}

    span = {0: pl.ds(0, Q_DEV), 1: pl.ds(0, half), 2: pl.ds(half, half)}

    def send_own(t, axis_place, step, to_a, to_b):
        axis = AXES[t][axis_place]
        for r in range(R):
            number = len(started)
            copy = pltpu.make_async_remote_copy(
                src_ref=q_ref.at[:, :, pl.ds(r * REGION_FEATURES + t * PART, PART)],
                dst_ref=g_ref.at[t, to_a, to_b, :, pl.ds(r * F, F)],
                send_sem=send_sem.at[number],
                recv_sem=recv_sem.at[number],
                device_id=(near[axis, step],),
                device_id_type=MESH,
            )
            copy.start()
            started.append(copy)
            arrivals[t, to_a, to_b, 3 + r] = copy

    def send(t, axis_place, step, da, db, to_a, to_b, piece):
        number = len(started)
        axis = AXES[t][axis_place]
        copy = pltpu.make_async_remote_copy(
            src_ref=g_ref.at[t, da, db, span[piece]],
            dst_ref=g_ref.at[t, to_a, to_b, span[piece]],
            send_sem=send_sem.at[number],
            recv_sem=recv_sem.at[number],
            device_id=(near[axis, step],),
            device_id_type=MESH,
        )
        copy.start()
        started.append(copy)
        arrivals[t, to_a, to_b, piece] = copy

    def have(t, a, b, piece=0):
        if (t, a, b, piece) in arrivals:
            arrivals[t, a, b, piece].wait_recv()
        else:
            for r in range(R):
                arrivals[t, a, b, 3 + r].wait_recv()

    def out_b(t, da):
        if da == 0:
            send_own(t, 1, 1, 0, 3)
            send_own(t, 1, 3, 0, 1)
        else:
            send(t, 1, 1, da, 0, da, 3, 0)
            send(t, 1, 3, da, 0, da, 1, 0)

    def on_b(t, da):
        have(t, da, 3)
        send(t, 1, 1, da, 3, da, 2, 1)
        have(t, da, 1)
        send(t, 1, 3, da, 1, da, 2, 2)

    id_copies = []

    def send_ids(first, count, peers):
        made = []
        for peer in peers:
            number = len(id_copies)
            copy = pltpu.make_async_remote_copy(
                src_ref=table_ref.at[pl.ds(first, count)],
                dst_ref=table_ref.at[pl.ds(first, count)],
                send_sem=id_send.at[number],
                recv_sem=id_recv.at[number],
                device_id=(peer,),
                device_id_type=MESH,
            )
            copy.start()
            made.append(copy)
            id_copies.append(copy)
        return made

    def line(axis):
        return [near[axis, step] for step in (1, 2, 3)]

    thirds = range(3)
    own_ids.wait()
    wave = send_ids(me, 1, [sibling])
    for t in thirds:
        send_own(t, 0, 1, 3, 0)
        send_own(t, 0, 3, 1, 0)
    for copy in wave:
        copy.wait_recv()
    wave = send_ids(me - core, 2, line(2))
    for t in thirds:
        out_b(t, 0)
    for copy in own:
        copy.start()
    for t in thirds:
        have(t, 3, 0)
        send(t, 0, 1, 3, 0, 2, 0, 1)
        have(t, 1, 0)
        send(t, 0, 3, 1, 0, 2, 0, 2)
    for t in thirds:
        out_b(t, 3)
        out_b(t, 1)
    for t in thirds:
        on_b(t, 0)
    for copy in wave:
        copy.wait_recv()
    wave = send_ids((me // 8) * 8, 8, line(1))
    for t in thirds:
        have(t, 2, 0, 1)
        have(t, 2, 0, 2)
        out_b(t, 2)
    for t in thirds:
        on_b(t, 3)
    for copy in wave:
        copy.wait_recv()
    wave = send_ids((me // 32) * 32, 32, line(0))
    for t in thirds:
        on_b(t, 1)
    for copy in wave:
        copy.wait_recv()
    make_tables()
    for t in thirds:
        on_b(t, 2)
    for copy in own:
        copy.wait()

    def the_rest():
        for t in thirds:
            for da in range(4):
                have(t, da, 2, 1)
                have(t, da, 2, 2)

    def all_sent():
        for copy in started + id_copies:
            copy.wait_send()

    return the_rest, all_sent


COPIES = 108
RING = 4
LAG = 3
BLOCKS = SIDE * SIDE


def frame_map(sim):
    best = sim[:, 0:F]
    for s in range(1, R):
        best = jnp.maximum(best, sim[:, s * F : (s + 1) * F])
    total = best[0:F]
    for r in range(1, R):
        total = total + best[r * F : (r + 1) * F]
    return total * (1.0 / (math.sqrt(REGION_FEATURES) * R))


def offsets_at(step):
    far = step // 12
    third = step % 3
    return (1 - far) * (step // 3) + far * (step - 12), (1 - far) * (third + third // 2) + far * 2


def score_kernel(
    q_ref, ids_ref, videos_ref, g_ref, rows_ref, map_ref,
    got_0, got_1, got_2, out, row, videos, sims, table, sel, wanted, sel_ref, wanted_ref,
    gather_send, gather_recv, local_sem, id_send, id_recv,
    got_sem, send_sem, recv_sem, self_sem, row_sem, video_sem, table_sem,
):
    got = (got_0, got_1, got_2)
    chip, core = position()
    me = device_at(chip, core)
    peers = [device_at(chip, core + 1)]
    for axis in range(3):
        for step in (1, 2, 3):
            for other in (0, 1):
                peers.append(device_at(shifted(chip, axis, step), core + other))
    load_videos = [
        pltpu.make_async_copy(
            videos_ref.at[:, :, pl.ds(r * REGION_FEATURES, REGION_FEATURES)],
            videos.at[:, pl.ds(r * F, F)],
            video_sem.at[r],
        )
        for r in range(R)
    ]

    def make_tables():
        lane = lax.broadcasted_iota(jnp.int32, (1, Q_DEV * K), 1)
        lanes = lax.broadcasted_iota(jnp.int32, (8, Q_DEV * K), 1)
        places = lax.broadcasted_iota(jnp.int32, (8, Q_DEV * K), 0)

        def one_source(source, carry):
            ids = table[source]
            key = lane * IDX_DEV + ids % IDX_DEV
            mine = ids // IDX_DEV == me
            low = jnp.min(jnp.where(mine, key, Q_DEV * K * IDX_DEV), axis=1, keepdims=True)
            high = jnp.max(jnp.where(mine, key, 0), axis=1, keepdims=True)
            wanted[source] = jnp.where(lane == 0, low % IDX_DEV, high % IDX_DEV)
            return carry

        lax.fori_loop(0, DEVICES, one_source, 0, unroll=8)

        for t in range(3):
            a, b, c = AXES[t]
            spots = shifted(chip, c, places // 2)
            target = device_at(spots, core + places % 2)

            def one_block(step, carry):
                da, db = offsets_at(step)
                source = device_at(shifted(shifted(chip, a, da), b, db), core)
                hit = jnp.broadcast_to(table[source] // IDX_DEV, (8, Q_DEV * K)) == target
                first = jnp.min(jnp.where(hit, lanes // K, Q_DEV - 1), axis=1, keepdims=True)
                last = jnp.max(jnp.where(hit, lanes // K, 0), axis=1, keepdims=True)
                sel[t * BLOCKS + step] = jnp.where(lanes == 0, first, last)
                return carry

            lax.fori_loop(0, BLOCKS, one_block, 0, unroll=4)
        moves = [
            pltpu.make_async_copy(wanted, wanted_ref, table_sem.at[0]),
            pltpu.make_async_copy(sel, sel_ref, table_sem.at[1]),
        ]
        for move in moves:
            move.start()
        for move in moves:
            move.wait()

    greet(peers)
    the_rest, all_sent = gather(
        chip, core, q_ref, ids_ref, g_ref, table, make_tables,
        gather_send, gather_recv, local_sem, id_send, id_recv,
    )
    for copy in load_videos:
        copy.start()

    def fetch(block, t):
        da, db = offsets_at(block)
        return pltpu.make_async_copy(g_ref.at[t, da, db], got[t], got_sem.at[t])

    def copies(block, t):
        slot = t * RING + block % RING
        made = []
        for step in range(4):
            for other in (0, 1):
                n = step * 2 + other
                if n > 0:
                    made.append(
                        pltpu.make_async_remote_copy(
                            src_ref=out.at[slot, n],
                            dst_ref=rows_ref.at[t, block, n],
                            send_sem=send_sem.at[slot, n],
                            recv_sem=recv_sem.at[t, block, n],
                            device_id=(device_at(shifted(chip, AXES[t][2], step), core + other),),
                            device_id_type=MESH,
                        )
                    )
        return made

    def keep(block, t):
        slot = t * RING + block % RING
        return pltpu.make_async_copy(out.at[slot, 0], rows_ref.at[t, block, 0], self_sem.at[slot])

    def load_row(block, t):
        return pltpu.make_async_copy(rows_ref.at[t, block], row.at[t], row_sem.at[t])

    def drain(block, t):
        for copy in copies(block, t):
            copy.wait_send()

    for t in range(3):
        fetch(0, t).start()

    def pack(block, t):
        @pl.when(block >= RING)
        def _():
            drain(block - RING, t)

        fetch(block, t).wait()
        slot = t * RING + block % RING
        for n in range(8):
            for rank in range(2):
                pick = sel_ref[t * BLOCKS + block, n, rank]
                out[slot, n, rank] = got[t][pick]
        for copy in copies(block, t):
            copy.start()
        keep(block, t).start()

        @pl.when(block < BLOCKS - 1)
        def _():
            fetch(block + 1, t).start()

    def receive(block, t):
        for copy in copies(block, t):
            copy.wait_recv()
        keep(block, t).wait()
        load_row(block, t).start()

    def add_up(block, t):
        load_row(block, t).wait()
        a, b, c = AXES[t]
        da, db = offsets_at(block)
        from_line = shifted(shifted(chip, a, da), b, db)

        for n in range(8):
            source = device_at(shifted(from_line, c, (4 - n // 2) % 4), core + n % 2)
            for rank in range(2):
                at = source * 2 + rank
                want = wanted_ref[source, 0, rank]
                sim = sims[at] + lax.dot_general(
                    row[t, n, rank],
                    videos[want, :, pl.ds(t * PART, PART)],
                    (((1,), (1,)), ((), ())),
                    preferred_element_type=jnp.float32,
                )
                sims[at] = sim
                map_ref[at] = frame_map(sim)

    def one_block(block, carry):
        @pl.when(block == LAG)
        def _():
            sims[...] = jnp.zeros_like(sims)
            for copy in load_videos:
                copy.wait()

        @pl.when(block == 11)
        def _():
            the_rest()

        for t in range(3):
            @pl.when(block < BLOCKS)
            def _():
                pack(block, t)

            @pl.when(jnp.logical_and(block > LAG, block <= BLOCKS + LAG))
            def _():
                add_up(block - LAG - 1, t)

            @pl.when(jnp.logical_and(block >= LAG, block < BLOCKS + LAG))
            def _():
                receive(block - LAG, t)

        return carry

    lax.fori_loop(0, BLOCKS + LAG + 1, one_block, 0)
    for t in range(3):
        for block in range(BLOCKS - RING, BLOCKS):
            drain(block, t)

    all_sent()


def conv_same(x, w):
    return lax.conv_general_dilated(
        x, w, (1, 1), "SAME", dimension_numbers=("NCHW", "OIHW", "NCHW"), preferred_element_type=jnp.float32
    )


def pool_two(x):
    b, c, h, w = x.shape
    return jnp.max(x.reshape(b, c, h // 2, 2, w // 2, 2), axis=(3, 5))


def body(queries, index_videos, candidates, conv_one, conv_two, conv_three):
    pairs = Q_DEV * K

    flat = candidates.reshape(pairs)
    _, _, maps = pl.pallas_call(
        score_kernel,
        out_shape=(
            jax.ShapeDtypeStruct((3, SIDE, SIDE, Q_DEV, FR, PART), jnp.bfloat16),
            jax.ShapeDtypeStruct((3, BLOCKS, 8, 2, FR, PART), jnp.bfloat16),
            jax.ShapeDtypeStruct((SLOTS, F, F), jnp.float32),
        ),
        in_specs=[pl.BlockSpec(memory_space=pl.ANY)] * 3,
        out_specs=(
            pl.BlockSpec(memory_space=pl.ANY),
            pl.BlockSpec(memory_space=pl.ANY),
            pl.BlockSpec(memory_space=pltpu.VMEM),
        ),
        scratch_shapes=[
            pltpu.VMEM((Q_DEV, FR, PART), jnp.bfloat16),
            pltpu.VMEM((Q_DEV, FR, PART), jnp.bfloat16),
            pltpu.VMEM((Q_DEV, FR, PART), jnp.bfloat16),
            pltpu.VMEM((3 * RING, 8, 2, FR, PART), jnp.bfloat16),
            pltpu.VMEM((3, 8, 2, FR, PART), jnp.bfloat16),
            pltpu.VMEM((IDX_DEV, FR, REGION_FEATURES), jnp.bfloat16),
            pltpu.VMEM((SLOTS, FR, FR), jnp.float32),
            pltpu.VMEM((DEVICES, 1, pairs), jnp.int32),
            pltpu.VMEM((3 * BLOCKS, 8, pairs), jnp.int32),
            pltpu.VMEM((DEVICES, 1, pairs), jnp.int32),
            pltpu.SMEM((3 * BLOCKS, 8, pairs), jnp.int32),
            pltpu.SMEM((DEVICES, 1, pairs), jnp.int32),
            pltpu.SemaphoreType.DMA((COPIES,)),
            pltpu.SemaphoreType.DMA((COPIES,)),
            pltpu.SemaphoreType.DMA((4, R)),
            pltpu.SemaphoreType.DMA((10,)),
            pltpu.SemaphoreType.DMA((10,)),
            pltpu.SemaphoreType.DMA((3,)),
            pltpu.SemaphoreType.DMA((3 * RING, 8)),
            pltpu.SemaphoreType.DMA((3, BLOCKS, 8)),
            pltpu.SemaphoreType.DMA((3 * RING,)),
            pltpu.SemaphoreType.DMA((3,)),
            pltpu.SemaphoreType.DMA((R,)),
            pltpu.SemaphoreType.DMA((2,)),
        ],
        compiler_params=pltpu.CompilerParams(
            collective_id=0, has_side_effects=True, vmem_limit_bytes=56 << 20
        ),
        name="score",
    )(queries, flat.reshape(1, 1, pairs), index_videos)

    frames = maps.reshape(SLOTS, 1, F, F).astype(jnp.bfloat16)
    first = pool_two(jax.nn.relu(conv_same(frames, conv_one))).astype(jnp.bfloat16)
    second = pool_two(jax.nn.relu(conv_same(first, conv_two))).astype(jnp.bfloat16)
    final = conv_same(second, conv_three)[:, 0]
    scores = jnp.mean(jnp.max(jnp.clip(final, -1.0, 1.0), axis=2), axis=1)

    back = lax.all_to_all(scores.reshape(DEVICES, 2), "shard", split_axis=0, concat_axis=0, tiled=True)
    my_holder = flat // IDX_DEV
    same = my_holder[:, None] == my_holder[None, :]
    earlier = jnp.arange(pairs)[None, :] < jnp.arange(pairs)[:, None]
    second_one = jnp.any(same & earlier, axis=1)
    to_me = my_holder[:, None] == jnp.arange(DEVICES)[None, :]
    score_first = jnp.sum(jnp.where(to_me, back[None, :, 0], 0.0), axis=1)
    score_last = jnp.sum(jnp.where(to_me, back[None, :, 1], 0.0), axis=1)
    return jnp.where(second_one, score_last, score_first).reshape(Q_DEV, K)


def solution(mesh):
    placed = (P("shard", None, None), P("shard", None, None), P("shard", None), P(), P(), P())
    return jax.shard_map(
        body, mesh=mesh, in_specs=placed, out_specs=P("shard", None), check_vma=False
    )
```

```python
import functools
import math

import jax
import jax.numpy as jnp
from jax import lax
from jax.experimental import pallas as pl
from jax.experimental.pallas import tpu as pltpu
from jax.sharding import PartitionSpec as P

MESH = pl.DeviceIdType.MESH
F = 8
R = 5
REGION_FEATURES = 1920
WIDTH = R * REGION_FEATURES
PART = REGION_FEATURES // 3
FR = F * R
SIDE = 4
Q_DEV = 16
K = 8
DEVICES = 128
IDX_DEV = 128
SLOTS = 2 * DEVICES
AXES = ((0, 1, 2), (1, 2, 0), (2, 0, 1))


def position():
    i = lax.axis_index("shard")
    return (i // 32, (i // 8) % 4, (i // 2) % 4), i % 2


def device_at(chip, core):
    return ((chip[0] % 4) * 4 + chip[1] % 4) * 8 + (chip[2] % 4) * 2 + core % 2


def shifted(chip, axis, step):
    moved = list(chip)
    moved[axis] = moved[axis] + step
    return tuple(moved)


def greet(peers):
    barrier = pltpu.get_barrier_semaphore()
    for peer in peers:
        pl.semaphore_signal(barrier, inc=1, device_id=(peer,), device_id_type=MESH)
    pl.semaphore_wait(barrier, len(peers))


def gather(chip, core, q_ref, ids_ref, g_ref, table_ref, make_tables, send_sem, recv_sem, local_sem, id_send, id_recv):
    near = {
        (axis, step): device_at(shifted(chip, axis, step), core) for axis in range(3) for step in (1, 2, 3)
    }
    sibling = device_at(chip, core + 1)
    half = Q_DEV // 2
    own = []
    for t in range(3):
        for r in range(R):
            copy = pltpu.make_async_copy(
                q_ref.at[:, :, pl.ds(r * REGION_FEATURES + t * PART, PART)],
                g_ref.at[t, 0, 0, :, pl.ds(r * F, F)],
                local_sem.at[t, r],
            )
            own.append(copy)
    me = device_at(chip, core)
    own_ids = pltpu.make_async_copy(ids_ref, table_ref.at[pl.ds(me, 1)], local_sem.at[3, 0])
    own_ids.start()
    started = []
    arrivals = {}

    span = {0: pl.ds(0, Q_DEV), 1: pl.ds(0, half), 2: pl.ds(half, half)}

    def send_own(t, axis_place, step, to_a, to_b):
        axis = AXES[t][axis_place]
        for r in range(R):
            number = len(started)
            copy = pltpu.make_async_remote_copy(
                src_ref=q_ref.at[:, :, pl.ds(r * REGION_FEATURES + t * PART, PART)],
                dst_ref=g_ref.at[t, to_a, to_b, :, pl.ds(r * F, F)],
                send_sem=send_sem.at[number],
                recv_sem=recv_sem.at[number],
                device_id=(near[axis, step],),
                device_id_type=MESH,
            )
            copy.start()
            started.append(copy)
            arrivals[t, to_a, to_b, 3 + r] = copy

    def send(t, axis_place, step, da, db, to_a, to_b, piece):
        number = len(started)
        axis = AXES[t][axis_place]
        copy = pltpu.make_async_remote_copy(
            src_ref=g_ref.at[t, da, db, span[piece]],
            dst_ref=g_ref.at[t, to_a, to_b, span[piece]],
            send_sem=send_sem.at[number],
            recv_sem=recv_sem.at[number],
            device_id=(near[axis, step],),
            device_id_type=MESH,
        )
        copy.start()
        started.append(copy)
        arrivals[t, to_a, to_b, piece] = copy

    def have(t, a, b, piece=0):
        if (t, a, b, piece) in arrivals:
            arrivals[t, a, b, piece].wait_recv()
        else:
            for r in range(R):
                arrivals[t, a, b, 3 + r].wait_recv()

    def out_b(t, da):
        if da == 0:
            send_own(t, 1, 1, 0, 3)
            send_own(t, 1, 3, 0, 1)
        else:
            send(t, 1, 1, da, 0, da, 3, 0)
            send(t, 1, 3, da, 0, da, 1, 0)

    def on_b(t, da):
        have(t, da, 3)
        send(t, 1, 1, da, 3, da, 2, 1)
        have(t, da, 1)
        send(t, 1, 3, da, 1, da, 2, 2)

    id_copies = []

    def send_ids(first, count, peers):
        made = []
        for peer in peers:
            number = len(id_copies)
            copy = pltpu.make_async_remote_copy(
                src_ref=table_ref.at[pl.ds(first, count)],
                dst_ref=table_ref.at[pl.ds(first, count)],
                send_sem=id_send.at[number],
                recv_sem=id_recv.at[number],
                device_id=(peer,),
                device_id_type=MESH,
            )
            copy.start()
            made.append(copy)
            id_copies.append(copy)
        return made

    def line(axis):
        return [near[axis, step] for step in (1, 2, 3)]

    thirds = range(3)
    own_ids.wait()
    wave = send_ids(me, 1, [sibling])
    for t in thirds:
        send_own(t, 0, 1, 3, 0)
        send_own(t, 0, 3, 1, 0)
    for copy in wave:
        copy.wait_recv()
    wave = send_ids(me - core, 2, line(2))
    for t in thirds:
        out_b(t, 0)
    for copy in own:
        copy.start()
    for t in thirds:
        have(t, 3, 0)
        send(t, 0, 1, 3, 0, 2, 0, 1)
        have(t, 1, 0)
        send(t, 0, 3, 1, 0, 2, 0, 2)
    for t in thirds:
        out_b(t, 3)
        out_b(t, 1)
    for t in thirds:
        on_b(t, 0)
    for copy in wave:
        copy.wait_recv()
    wave = send_ids((me // 8) * 8, 8, line(1))
    for t in thirds:
        have(t, 2, 0, 1)
        have(t, 2, 0, 2)
        out_b(t, 2)
    for t in thirds:
        on_b(t, 3)
    for copy in wave:
        copy.wait_recv()
    wave = send_ids((me // 32) * 32, 32, line(0))
    for t in thirds:
        on_b(t, 1)
    for copy in wave:
        copy.wait_recv()
    make_tables()
    for t in thirds:
        on_b(t, 2)
    for copy in own:
        copy.wait()

    def the_rest():
        for t in thirds:
            for da in range(4):
                have(t, da, 2, 1)
                have(t, da, 2, 2)

    def all_sent():
        for copy in started + id_copies:
            copy.wait_send()

    return the_rest, all_sent


COPIES = 108
RING = 4
LAG = 3
BLOCKS = SIDE * SIDE


def frame_map(sim):
    best = sim[:, 0:F]
    for s in range(1, R):
        best = jnp.maximum(best, sim[:, s * F : (s + 1) * F])
    total = best[0:F]
    for r in range(1, R):
        total = total + best[r * F : (r + 1) * F]
    return total * (1.0 / (math.sqrt(REGION_FEATURES) * R))


def offsets_at(step):
    far = step // 12
    third = step % 3
    return (1 - far) * (step // 3) + far * (step - 12), (1 - far) * (third + third // 2) + far * 2


def score_kernel(
    q_ref, ids_ref, videos_ref, g_ref, rows_ref, map_ref,
    got_0, got_1, got_2, out, row, videos, sims, table, sel, wanted, sel_ref, wanted_ref,
    gather_send, gather_recv, local_sem, id_send, id_recv,
    got_sem, send_sem, recv_sem, self_sem, row_sem, video_sem, table_sem,
):
    got = (got_0, got_1, got_2)
    chip, core = position()
    me = device_at(chip, core)
    peers = [device_at(chip, core + 1)]
    for axis in range(3):
        for step in (1, 2, 3):
            for other in (0, 1):
                peers.append(device_at(shifted(chip, axis, step), core + other))
    load_videos = [
        pltpu.make_async_copy(
            videos_ref.at[:, :, pl.ds(r * REGION_FEATURES, REGION_FEATURES)],
            videos.at[:, pl.ds(r * F, F)],
            video_sem.at[r],
        )
        for r in range(R)
    ]

    def make_tables():
        lane = lax.broadcasted_iota(jnp.int32, (1, Q_DEV * K), 1)
        lanes = lax.broadcasted_iota(jnp.int32, (8, Q_DEV * K), 1)
        places = lax.broadcasted_iota(jnp.int32, (8, Q_DEV * K), 0)

        def one_source(source, carry):
            ids = table[source]
            key = lane * IDX_DEV + ids % IDX_DEV
            mine = ids // IDX_DEV == me
            low = jnp.min(jnp.where(mine, key, Q_DEV * K * IDX_DEV), axis=1, keepdims=True)
            high = jnp.max(jnp.where(mine, key, 0), axis=1, keepdims=True)
            wanted[source] = jnp.where(lane == 0, low % IDX_DEV, high % IDX_DEV)
            return carry

        lax.fori_loop(0, DEVICES, one_source, 0, unroll=8)

        for t in range(3):
            a, b, c = AXES[t]
            spots = shifted(chip, c, places // 2)
            target = device_at(spots, core + places % 2)

            def one_block(step, carry):
                da, db = offsets_at(step)
                source = device_at(shifted(shifted(chip, a, da), b, db), core)
                hit = jnp.broadcast_to(table[source] // IDX_DEV, (8, Q_DEV * K)) == target
                first = jnp.min(jnp.where(hit, lanes // K, Q_DEV - 1), axis=1, keepdims=True)
                last = jnp.max(jnp.where(hit, lanes // K, 0), axis=1, keepdims=True)
                sel[t * BLOCKS + step] = jnp.where(lanes == 0, first, last)
                return carry

            lax.fori_loop(0, BLOCKS, one_block, 0, unroll=4)
        moves = [
            pltpu.make_async_copy(wanted, wanted_ref, table_sem.at[0]),
            pltpu.make_async_copy(sel, sel_ref, table_sem.at[1]),
        ]
        for move in moves:
            move.start()
        for move in moves:
            move.wait()

    greet(peers)
    the_rest, all_sent = gather(
        chip, core, q_ref, ids_ref, g_ref, table, make_tables,
        gather_send, gather_recv, local_sem, id_send, id_recv,
    )
    for copy in load_videos:
        copy.start()

    def fetch(block, t):
        da, db = offsets_at(block)
        return pltpu.make_async_copy(g_ref.at[t, da, db], got[t], got_sem.at[t])

    def copies(block, t):
        slot = t * RING + block % RING
        made = []
        for step in range(4):
            for other in (0, 1):
                n = step * 2 + other
                if n > 0:
                    made.append(
                        pltpu.make_async_remote_copy(
                            src_ref=out.at[slot, n],
                            dst_ref=rows_ref.at[t, block, n],
                            send_sem=send_sem.at[slot, n],
                            recv_sem=recv_sem.at[t, block, n],
                            device_id=(device_at(shifted(chip, AXES[t][2], step), core + other),),
                            device_id_type=MESH,
                        )
                    )
        return made

    def keep(block, t):
        slot = t * RING + block % RING
        return pltpu.make_async_copy(out.at[slot, 0], rows_ref.at[t, block, 0], self_sem.at[slot])

    def load_row(block, t):
        return pltpu.make_async_copy(rows_ref.at[t, block], row.at[t], row_sem.at[t])

    def drain(block, t):
        for copy in copies(block, t):
            copy.wait_send()

    for t in range(3):
        fetch(0, t).start()

    def pack(block, t):
        @pl.when(block >= RING)
        def _():
            drain(block - RING, t)

        fetch(block, t).wait()
        slot = t * RING + block % RING
        for n in range(8):
            for rank in range(2):
                pick = sel_ref[t * BLOCKS + block, n, rank]
                out[slot, n, rank] = got[t][pick]
        for copy in copies(block, t):
            copy.start()
        keep(block, t).start()

        @pl.when(block < BLOCKS - 1)
        def _():
            fetch(block + 1, t).start()

    def receive(block, t):
        for copy in copies(block, t):
            copy.wait_recv()
        keep(block, t).wait()
        load_row(block, t).start()

    def add_up(block, t):
        load_row(block, t).wait()
        a, b, c = AXES[t]
        da, db = offsets_at(block)
        from_line = shifted(shifted(chip, a, da), b, db)

        for n in range(8):
            source = device_at(shifted(from_line, c, (4 - n // 2) % 4), core + n % 2)
            for rank in range(2):
                at = source * 2 + rank
                want = wanted_ref[source, 0, rank]
                sim = sims[at] + lax.dot_general(
                    row[t, n, rank],
                    videos[want, :, pl.ds(t * PART, PART)],
                    (((1,), (1,)), ((), ())),
                    preferred_element_type=jnp.float32,
                )
                sims[at] = sim
                map_ref[at] = frame_map(sim)

    def one_block(block, carry):
        @pl.when(block == LAG)
        def _():
            sims[...] = jnp.zeros_like(sims)
            for copy in load_videos:
                copy.wait()

        @pl.when(block == 11)
        def _():
            the_rest()

        for t in range(3):
            @pl.when(block < BLOCKS)
            def _():
                pack(block, t)

            @pl.when(jnp.logical_and(block > LAG, block <= BLOCKS + LAG))
            def _():
                add_up(block - LAG - 1, t)

            @pl.when(jnp.logical_and(block >= LAG, block < BLOCKS + LAG))
            def _():
                receive(block - LAG, t)

        return carry

    lax.fori_loop(0, BLOCKS + LAG + 1, one_block, 0)
    for t in range(3):
        for block in range(BLOCKS - RING, BLOCKS):
            drain(block, t)

    all_sent()


def return_kernel(give_ref, out_ref, middle, send_sem, recv_sem, own_sem):
    chip, core = position()
    z, x, y = chip
    pillar = z * 4 + x
    spot = y * 2 + core
    far = [(step, (pillar + step) % 16) for step in range(1, 16)]
    near = [(step, (spot + step) % 8) for step in range(1, 8)]
    greet([at * 8 + spot for _, at in far] + [pillar * 8 + at for _, at in near])

    def hop(first, moves, own_source, target):
        made = []
        for i, (source, peer) in enumerate(moves):
            made.append(
                pltpu.make_async_remote_copy(
                    src_ref=source,
                    dst_ref=target,
                    send_sem=send_sem.at[first + i],
                    recv_sem=recv_sem.at[first + i],
                    device_id=(peer,),
                    device_id_type=MESH,
                )
            )
        own = pltpu.make_async_copy(own_source, target, own_sem)
        for copy in made:
            copy.start()
        own.start()
        own.wait()
        for copy in made:
            copy.wait_recv()
        return made

    sent = hop(
        0, [(give_ref.at[at], at * 8 + spot) for _, at in far], give_ref.at[pillar], middle.at[pillar]
    )
    sent += hop(
        15, [(middle.at[:, at], pillar * 8 + at) for _, at in near], middle.at[:, spot], out_ref.at[spot]
    )
    for copy in sent:
        copy.wait_send()


def conv_same(x, w):
    return lax.conv_general_dilated(
        x, w, (1, 1), "SAME", dimension_numbers=("NCHW", "OIHW", "NCHW"), preferred_element_type=jnp.float32
    )


def pool_two(x):
    b, c, h, w = x.shape
    return jnp.max(x.reshape(b, c, h // 2, 2, w // 2, 2), axis=(3, 5))


def body(queries, index_videos, candidates, conv_one, conv_two, conv_three):
    pairs = Q_DEV * K

    flat = candidates.reshape(pairs)
    _, _, maps = pl.pallas_call(
        score_kernel,
        out_shape=(
            jax.ShapeDtypeStruct((3, SIDE, SIDE, Q_DEV, FR, PART), jnp.bfloat16),
            jax.ShapeDtypeStruct((3, BLOCKS, 8, 2, FR, PART), jnp.bfloat16),
            jax.ShapeDtypeStruct((SLOTS, F, F), jnp.float32),
        ),
        in_specs=[pl.BlockSpec(memory_space=pl.ANY)] * 3,
        out_specs=(
            pl.BlockSpec(memory_space=pl.ANY),
            pl.BlockSpec(memory_space=pl.ANY),
            pl.BlockSpec(memory_space=pltpu.VMEM),
        ),
        scratch_shapes=[
            pltpu.VMEM((Q_DEV, FR, PART), jnp.bfloat16),
            pltpu.VMEM((Q_DEV, FR, PART), jnp.bfloat16),
            pltpu.VMEM((Q_DEV, FR, PART), jnp.bfloat16),
            pltpu.VMEM((3 * RING, 8, 2, FR, PART), jnp.bfloat16),
            pltpu.VMEM((3, 8, 2, FR, PART), jnp.bfloat16),
            pltpu.VMEM((IDX_DEV, FR, REGION_FEATURES), jnp.bfloat16),
            pltpu.VMEM((SLOTS, FR, FR), jnp.float32),
            pltpu.VMEM((DEVICES, 1, pairs), jnp.int32),
            pltpu.VMEM((3 * BLOCKS, 8, pairs), jnp.int32),
            pltpu.VMEM((DEVICES, 1, pairs), jnp.int32),
            pltpu.SMEM((3 * BLOCKS, 8, pairs), jnp.int32),
            pltpu.SMEM((DEVICES, 1, pairs), jnp.int32),
            pltpu.SemaphoreType.DMA((COPIES,)),
            pltpu.SemaphoreType.DMA((COPIES,)),
            pltpu.SemaphoreType.DMA((4, R)),
            pltpu.SemaphoreType.DMA((10,)),
            pltpu.SemaphoreType.DMA((10,)),
            pltpu.SemaphoreType.DMA((3,)),
            pltpu.SemaphoreType.DMA((3 * RING, 8)),
            pltpu.SemaphoreType.DMA((3, BLOCKS, 8)),
            pltpu.SemaphoreType.DMA((3 * RING,)),
            pltpu.SemaphoreType.DMA((3,)),
            pltpu.SemaphoreType.DMA((R,)),
            pltpu.SemaphoreType.DMA((2,)),
        ],
        compiler_params=pltpu.CompilerParams(
            collective_id=0, has_side_effects=True, vmem_limit_bytes=56 << 20
        ),
        name="score",
    )(queries, flat.reshape(1, 1, pairs), index_videos)

    frames = maps.reshape(SLOTS, 1, F, F).astype(jnp.bfloat16)
    first = pool_two(jax.nn.relu(conv_same(frames, conv_one))).astype(jnp.bfloat16)
    second = pool_two(jax.nn.relu(conv_same(first, conv_two))).astype(jnp.bfloat16)
    final = conv_same(second, conv_three)[:, 0]
    scores = jnp.mean(jnp.max(jnp.clip(final, -1.0, 1.0), axis=2), axis=1)

    give = jnp.pad(scores.reshape(16, 8, 1, 2), ((0, 0), (0, 0), (0, 0), (0, pairs - 2)))
    back = pl.pallas_call(
        return_kernel,
        out_shape=jax.ShapeDtypeStruct((8, 16, 1, pairs), jnp.float32),
        in_specs=[pl.BlockSpec(memory_space=pltpu.VMEM)],
        out_specs=pl.BlockSpec(memory_space=pltpu.VMEM),
        scratch_shapes=[
            pltpu.VMEM((16, 8, 1, pairs), jnp.float32),
            pltpu.SemaphoreType.DMA((22,)),
            pltpu.SemaphoreType.DMA((22,)),
            pltpu.SemaphoreType.DMA,
        ],
        compiler_params=pltpu.CompilerParams(collective_id=1, has_side_effects=True),
        name="give_back",
    )(give)
    back = back.reshape(DEVICES, pairs)[:, :2]
    my_holder = flat // IDX_DEV
    same = my_holder[:, None] == my_holder[None, :]
    earlier = jnp.arange(pairs)[None, :] < jnp.arange(pairs)[:, None]
    second_one = jnp.any(same & earlier, axis=1)
    at = my_holder % 8 * 16 + my_holder // 8
    to_me = at[:, None] == jnp.arange(DEVICES)[None, :]
    score_first = jnp.sum(jnp.where(to_me, back[None, :, 0], 0.0), axis=1)
    score_last = jnp.sum(jnp.where(to_me, back[None, :, 1], 0.0), axis=1)
    return jnp.where(second_one, score_last, score_first).reshape(Q_DEV, K)


def solution(mesh):
    placed = (P("shard", None, None), P("shard", None, None), P("shard", None), P(), P(), P())
    return jax.shard_map(
        body, mesh=mesh, in_specs=placed, out_specs=P("shard", None), check_vma=False
    )
```
